32 devices in a mesh: ctx: 8 (over z, y), chan: 4 (over x, core).
Axes of the slice: x: 2, y: 2, z: 4, core: 2. Of those that a mesh axis runs over, the one named last changes fastest.
Arguments:
- tokens: bfloat16 [2048, 4096], P('ctx', 'chan'), may hold values from -6 to 6
- gain: float32 [4096], replicated, may hold values from 0.1 to 1.9
- in_weight: bfloat16 [3, 4096, 2048], P(None, None, 'chan'), may hold values from -0.09375 to 0.09375
- short_weight: float32 [3, 3, 2048], P(None, None, 'chan'), may hold values from -3.5 to 3.5
- residues: float32 [16, 2048], P(None, 'chan'), may hold values from -1.5 to 1.5
- rates: float32 [16, 2048], P(None, 'chan'), may hold values from 0.1 to 51
- out_weight: bfloat16 [2048, 4096], P('chan'), may hold values from -0.1875 to 0.1875
Outputs:
- mixed: bfloat16 [2048, 4096], P('ctx', 'chan')
The draws below stay inside these ranges and needn't reach their ends.
All inputs are finite; a program needn't handle non-finite values.
Results may differ from the reference program's by a relative error of at most 0.018.
Values may be sent and summed in bfloat16 or wider, within the bound.
A program may use at most 128 MiB of HBM per device.

```python
import math
import jax
import jax.numpy as jnp
from jax import lax

D = 4096
CH = 2048
MODES = 16
SHORT = 3
TOKENS = 2048


def draw_rates(key, part):
    grid_shape = (MODES, CH)
    top_rate = float(TOKENS // 40)
    values = jnp.exp(jax.random.uniform(key, grid_shape, jnp.float32, math.log(0.5), math.log(top_rate)))
    return jnp.clip(values, 0.1, top_rate)


def strengthened(values, stream_key, source, target, blocks, factor):
    def block_of(position):
        return (jnp.arange(values.shape[position]) // (values.shape[position] // blocks)).reshape((-1,) + (1,) * (values.ndim - 1 - position))

    first = jax.random.permutation(stream_key, blocks)[block_of(target)]
    other_side = (block_of(target) + blocks // 2) % blocks
    return jnp.where((block_of(source) == first) | (block_of(source) == other_side), factor * values, values)


def shard_levels(stream_key, dims, cuts, smallest, high):
    def one(axis_at, shards_of):
        heights = jax.random.uniform(jax.random.fold_in(jax.random.fold_in(stream_key, 6), axis_at), (shards_of,), jnp.float32, smallest / len(cuts), high / len(cuts))
        return jnp.repeat(jnp.exp(heights), dims[axis_at] // shards_of).reshape((-1,) + (1,) * (len(dims) - axis_at - 1))

    loudness = one(*cuts[0])
    for cut in cuts[1:]:
        loudness = loudness * one(*cut)
    return loudness


def gaussian(key, dims, width, bound, pieces=(), kind=jnp.bfloat16):
    values = width * jax.random.normal(key, dims, jnp.float32)
    if pieces:
        values = values * shard_levels(key, dims, pieces, -0.22, 0.18)
    return jnp.clip(values, -bound, bound).astype(kind)


def bell_draw_with(own_key, extent, deviation, bound, shards, heavy, held_as=jnp.bfloat16):
    entries = deviation * jax.random.normal(own_key, extent, jnp.float32)
    if shards:
        entries = entries * shard_levels(own_key, extent, shards, -0.22, 0.18)
    return jnp.clip(strengthened(entries, jax.random.fold_in(own_key, 3), *heavy), -bound, bound).astype(held_as)


def setup_inputs(seed: int = 0) -> dict:
    seeds = jax.random.split(jax.random.key(seed), 8)
    return {
        "tokens": gaussian(seeds[0], (TOKENS, D), 1.0, 6.0, ((0, 8), (1, 4))),
        "gain": jnp.clip(1.0 + 0.18 * jax.random.normal(seeds[1], (D,), jnp.float32), 0.1, 1.9),
        "in_weight": gaussian(seeds[2], (3, D, CH), D ** -0.5, 0.09375, ((2, 4),)),
        "short_weight": gaussian(seeds[3], (3, SHORT, CH), SHORT ** -0.5, 3.5, ((2, 4),), jnp.float32),
        "residues": gaussian(seeds[4], (MODES, CH), MODES ** -0.5, 1.5, ((1, 4),), jnp.float32),
        "rates": draw_rates(jax.random.fold_in(seeds[7], 71), 0),
        "out_weight": bell_draw_with(seeds[6], (CH, D), CH ** -0.5, 0.1875, ((0, 4),), (0, 1, 4, 2.0)),
    }


def reference(tokens, gain, in_weight, short_weight, residues, rates, out_weight):
    wide_rows = tokens.astype(jnp.float32)
    scale_rms = lax.rsqrt(lax.optimization_barrier(jnp.mean(wide_rows * wide_rows, axis=-1, keepdims=True)) + 1e-06)
    normed = (wide_rows * scale_rms * gain).astype(jnp.bfloat16)
    filtered = []
    for g in range(3):
        projected = jnp.dot(normed, in_weight[g], preferred_element_type=jnp.float32).astype(jnp.bfloat16)
        widened = projected.astype(jnp.float32)
        mixture = jnp.zeros_like(widened)
        for i in range(SHORT):
            shifted = jnp.pad(widened, ((i, 0), (0, 0)))[:TOKENS]
            mixture = mixture + short_weight[g, i][None, :] * shifted
        filtered.append(mixture)
    drive_term = filtered[1] * filtered[2]
    decay_rate = rates / TOKENS
    amplitude = residues * jnp.sqrt(-jnp.expm1(-2.0 * decay_rate))
    positions = jnp.arange(TOKENS, dtype=jnp.float32)[:, None]
    kernel = jnp.zeros((TOKENS, CH), jnp.float32)
    for m in range(MODES):
        kernel = kernel + amplitude[m][None, :] * jnp.exp(-decay_rate[m][None, :] * positions)
    padded_length = 2 * TOKENS
    product = jnp.fft.rfft(drive_term, n=padded_length, axis=0) * jnp.fft.rfft(kernel, n=padded_length, axis=0)
    convolved = jnp.fft.irfft(product, n=padded_length, axis=0)[:TOKENS]
    gated_rows = (filtered[0] * convolved).astype(jnp.bfloat16)
    return jnp.dot(gated_rows, out_weight, preferred_element_type=jnp.float32).astype(jnp.bfloat16)
```

```python
import math

import jax
import jax.numpy as jnp
from jax import lax
from jax.sharding import PartitionSpec as P

high = lax.Precision.HIGH


def from_behind(shard, axis, by):
    peers = lax.axis_size(axis)
    pairs = [(i, i + by) for i in range(peers) if 0 <= i + by < peers]
    return lax.ppermute(shard, axis, pairs)


def odd_tables(rows):
    steps = jnp.arange(rows, dtype=jnp.int32)
    turns = (2 * steps[:, None] + 1) * steps[None, :] % (4 * rows)
    angle = turns.astype(jnp.float32) * (math.pi / (2 * rows))
    return jnp.cos(angle), jnp.sin(angle)


def local_convolution(drive, kernel):
    rows = drive.shape[0]
    cos_table, sin_table = odd_tables(rows)
    forward = jnp.concatenate([cos_table, -sin_table], axis=0)
    both = jnp.concatenate([drive, kernel], axis=1)
    spectra = jnp.dot(forward, both, precision=high)
    width = drive.shape[1]
    dr, di = spectra[:rows, :width], spectra[rows:, :width]
    kr, ki = spectra[:rows, width:], spectra[rows:, width:]
    product = jnp.concatenate([dr * kr - di * ki, dr * ki + di * kr], axis=0)
    backward = jnp.concatenate([cos_table.T, -sin_table.T], axis=1) / rows
    return jnp.dot(backward, product, precision=high)


def shards(tokens, gain, in_weight, short_weight, residues, rates, out_weight):
    features_all = lax.all_gather(tokens, "chan", axis=1, tiled=True)
    wide_rows = features_all.astype(jnp.float32)
    scale_rms = lax.rsqrt(jnp.mean(wide_rows * wide_rows, axis=-1, keepdims=True) + 1e-06)
    normed = (wide_rows * scale_rms * gain).astype(jnp.bfloat16)
    projected = jnp.einsum(
        "td,gdc->gtc", normed, in_weight, preferred_element_type=jnp.float32
    ).astype(jnp.bfloat16)
    rows = projected.shape[1]
    rim_size = short_weight.shape[1] - 1
    rim_rows = from_behind(projected[:, rows - rim_size :, :], "ctx", 1)
    extended = jnp.concatenate([rim_rows, projected], axis=1).astype(jnp.float32)
    filtered = jnp.zeros((3, rows, projected.shape[2]), jnp.float32)
    for i in range(rim_size + 1):
        filtered = (
            filtered + short_weight[:, i][:, None, :] * extended[:, rim_size - i : rim_size - i + rows]
        )
    drive = filtered[1] * filtered[2]
    blocks = lax.axis_size("ctx")
    block = lax.axis_index("ctx")
    decay = rates / (rows * blocks)
    amplitude = residues * jnp.sqrt(-jnp.expm1(-2.0 * decay))
    steps = jnp.arange(rows, dtype=jnp.float32)[None, :, None]
    powers = jnp.exp(-decay[:, None, :] * steps)
    kernel = jnp.sum(amplitude[:, None, :] * powers, axis=0)
    state = jnp.sum(jnp.exp(-decay[:, None, :] * (rows - 1 - steps)) * drive[None], axis=1)
    states = lax.all_gather(state, "ctx", axis=0)
    behind = block - 1 - jnp.arange(blocks, dtype=jnp.int32)
    gaps = jnp.maximum(behind, 0).astype(jnp.float32)[:, None, None] * rows
    carried = jnp.where(behind[:, None, None] >= 0, jnp.exp(-decay[None] * gaps) * states, 0.0)
    carried = jnp.sum(carried, axis=0) * amplitude
    tail = jnp.sum(jnp.exp(-decay[:, None, :] * (steps + 1)) * carried[:, None, :], axis=0)
    convolved = local_convolution(drive, kernel) + tail
    gated_rows = (filtered[0] * convolved).astype(jnp.bfloat16)
    partial_sums = jnp.dot(gated_rows, out_weight, preferred_element_type=jnp.float32)
    return lax.psum_scatter(
        partial_sums.astype(jnp.bfloat16), "chan", scatter_dimension=1, tiled=True
    )


def solution(mesh):
    return jax.shard_map(
        shards,
        mesh=mesh,
        in_specs=(
            P("ctx", "chan"),
            P(),
            P(None, None, "chan"),
            P(None, None, "chan"),
            P(None, "chan"),
            P(None, "chan"),
            P("chan", None),
        ),
        out_specs=P("ctx", "chan"),
        check_vma=False,
    )
```

```python
import functools
import math

import jax
import jax.numpy as jnp
import numpy as np
from jax import lax
from jax.experimental import pallas as pl
from jax.experimental.pallas import tpu as pltpu
from jax.sharding import PartitionSpec as P

RIM = 16
MESH = pl.DeviceIdType.MESH
f32 = jnp.float32
bf16 = jnp.bfloat16


def tables(rows):
    steps = np.arange(rows)
    turns = ((2 * steps[:, None] + 1) * steps[None, :]) % (4 * rows)
    angle = turns * (math.pi / (2 * rows))
    cos, sin = np.cos(angle), np.sin(angle)
    forward = np.concatenate([cos, -sin], axis=0)
    flipped = np.eye(rows)[::-1]
    both = np.concatenate([forward, flipped], axis=0)
    backward = np.concatenate([cos.T, -sin.T], axis=1) / rows
    return forward.astype(np.float32), both.astype(np.float32), backward.astype(np.float32)


def one_less_exp(x):
    series = jnp.full_like(x, 1.0 / 5040.0)
    for term in (720.0, 120.0, 24.0, 6.0, 2.0, 1.0):
        series = 1.0 / term - x * series
    return jnp.where(x < 0.25, x * series, 1.0 - jnp.exp(-x))


def layer(
    n_ctx,
    tok,
    gain,
    w_hbm,
    short,
    residues,
    rates,
    ow_hbm,
    fwd_hbm,
    both_hbm,
    back_hbm,
    out,
    buf,
    w,
    ow,
    fwd,
    both,
    back,
    acc,
    squares,
    ext,
    gate,
    powers,
    spec_k,
    spec,
    drive,
    conv,
    amp,
    state_out,
    state_in,
    carry,
    gated,
    gated_in,
    sent,
    landed,
    local_sem,
    g_send,
    g_recv,
    h_send,
    h_recv,
    o_send,
    o_recv,
    s_send,
    s_recv,
    r_send,
    r_recv,
):
    rows, width = tok.shape
    chans = w_hbm.shape[2]
    modes = rates.shape[0]
    cut = width // 4
    length = rows * n_ctx
    me = lax.axis_index("chan")
    ctx = lax.axis_index("ctx")
    sib = me + 1 - 2 * lax.rem(me, 2)
    acr = lax.rem(me + 2, 4)
    dia = lax.rem(sib + 2, 4)
    owners = (me, sib, acr, dia)

    def local(src, dst, k):
        copy = pltpu.make_async_copy(src, dst, local_sem.at[k])
        copy.start()
        return copy

    def remote(src, dst, send, recv, peer):
        return pltpu.make_async_remote_copy(
            src_ref=src, dst_ref=dst, send_sem=send, recv_sem=recv, device_id=peer, device_id_type=MESH
        )

    def cols(block, size):
        return pl.ds(pl.multiple_of(block * size, size), size)

    own_tokens = local(tok, buf.at[0, 0:rows], 0)
    fwd_copy = local(fwd_hbm, fwd, 1)
    w_copies = [
        local(w_hbm.at[:, cols(owners[s], width), :], w.at[:, s * width : (s + 1) * width, :], 2 + s)
        for s in range(4)
    ]
    both_copy = local(both_hbm, both, 6)
    back_copy = local(back_hbm, back, 7)
    ow_copies = [local(ow_hbm.at[:, cols(b, width)], ow.at[0, i], 8 + i) for i, b in enumerate((me, acr))]

    barrier = pltpu.get_barrier_semaphore()
    pl.semaphore_signal(barrier, inc=1, device_id={"chan": sib}, device_id_type=MESH)
    pl.semaphore_signal(barrier, inc=1, device_id={"chan": acr}, device_id_type=MESH)
    for rel in range(1, n_ctx):
        peer = lax.rem(ctx + rel, n_ctx)
        pl.semaphore_signal(barrier, inc=1, device_id={"ctx": peer}, device_id_type=MESH)
    pl.semaphore_wait(barrier, n_ctx + 1)

    across = []
    for c in range(4):
        here = slice(c * cut, (c + 1) * cut)
        across.append(
            remote(tok.at[:, here], buf.at[2, 0:rows, here], g_send.at[c], g_recv.at[c], {"chan": acr})
        )
    beside = remote(tok, buf.at[1, 0:rows], g_send.at[4], g_recv.at[4], {"chan": sib})
    rim_on = remote(
        tok.at[rows - RIM : rows, :],
        buf.at[0, rows : rows + RIM],
        h_send.at[0],
        h_recv.at[0],
        {"ctx": lax.rem(ctx + 1, n_ctx)},
    )
    rim_on.start()
    across[0].start()
    beside.start()
    rim_here = buf.at[0, rows : rows + RIM]
    rim_on.wait_recv()
    rim_across = remote(rim_here, buf.at[2, rows : rows + RIM], h_send.at[1], h_recv.at[1], {"chan": acr})
    rim_beside = remote(rim_here, buf.at[1, rows : rows + RIM], h_send.at[2], h_recv.at[2], {"chan": sib})
    rim_across.start()
    rim_beside.start()
    for c in range(1, 4):
        across[c].start()
    ow_out = []
    for i, b in enumerate((sib, dia)):
        copy = remote(ow_hbm.at[:, cols(b, width)], ow.at[1, i], o_send.at[i], o_recv.at[i], {"chan": sib})
        copy.start()
        ow_out.append(copy)

    decay_all = rates[...] * (1.0 / length)
    amp[...] = residues[...] * jnp.sqrt(one_less_exp(2.0 * decay_all))
    conv[...] = jnp.zeros_like(conv)
    eighth = lax.broadcasted_iota(jnp.int32, (8, chans), 0).astype(f32)
    groups = lax.broadcasted_iota(jnp.int32, (rows // 8, chans), 0).astype(f32) * 8.0

    def build(m, _):
        decay = rates[pl.ds(m, 1), :] * (1.0 / length)
        fine = jnp.exp(-decay * eighth)
        coarse = jnp.exp(-decay * groups)
        strength = amp[pl.ds(m, 1), :]
        for a in range(rows // 8):
            here = slice(a * 8, a * 8 + 8)
            value = fine * coarse[a : a + 1, :]
            powers[m, here, :] = value
            conv[here, :] += strength * value
        return 0

    lax.fori_loop(0, modes, build, 0)

    squares[...] = jnp.zeros_like(squares)

    def accumulate(slot, start, size, first):
        x = buf[slot, :, start : start + size].astype(f32)
        part = squares[...]
        for k in range(0, size, 128):
            piece = x[:, k : k + 128]
            part = part + piece * piece
        squares[...] = part
        scaled = (x * gain[pl.ds(owners[slot], 1), start : start + size]).astype(bf16)
        for g in range(3):
            base = slot * width + start
            term = jnp.dot(scaled, w[g, base : base + size, :], preferred_element_type=f32)
            if first:
                acc[g] = term
            else:
                acc[g] += term

    own_tokens.wait()
    w_copies[0].wait()
    accumulate(0, 0, width, True)
    across[0].wait_recv()
    onward = [
        remote(
            buf.at[2, 0:rows, c * cut : (c + 1) * cut],
            buf.at[3, 0:rows, c * cut : (c + 1) * cut],
            g_send.at[5 + c],
            g_recv.at[5 + c],
            {"chan": sib},
        )
        for c in range(4)
    ]
    onward[0].start()
    rim_across.wait_recv()
    rim_onward = remote(
        buf.at[2, rows : rows + RIM], buf.at[3, rows : rows + RIM], h_send.at[3], h_recv.at[3], {"chan": sib}
    )
    rim_onward.start()
    rim_beside.wait_recv()
    beside.wait_recv()
    w_copies[1].wait()
    accumulate(1, 0, width, False)

    fwd_copy.wait()
    spec_k[...] = jnp.dot(
        fwd[...], conv[...], preferred_element_type=f32, precision=lax.Precision.HIGHEST
    )

    w_copies[2].wait()
    w_copies[3].wait()
    for c in range(4):
        if c:
            across[c].wait_recv()
            onward[c].start()
        accumulate(2, c * cut, cut, False)
        if c == 0:
            rim_onward.wait_recv()
        onward[c].wait_recv()
        accumulate(3, c * cut, cut, False)

    mean = jnp.sum(squares[...], axis=1, keepdims=True) * (1.0 / (4 * width))
    scale = lax.rsqrt(mean + 1e-06)
    keep = jnp.where(ctx > 0, 1.0, 0.0)
    for g in range(3):
        ext[g, 0:8, :] = (acc[g, rows + 8 : rows + 16, :] * scale[rows + 8 : rows + 16]).astype(bf16).astype(
            f32
        ) * keep
        ext[g, 8 : rows + 8, :] = (acc[g, 0:rows, :] * scale[0:rows]).astype(bf16).astype(f32)
    step = 64
    for r in range(0, rows, step):
        mixed = []
        for g in range(3):
            total = short[g, 0:1, :] * ext[g, r + 8 : r + 8 + step, :]
            total = total + short[g, 1:2, :] * ext[g, r + 7 : r + 7 + step, :]
            total = total + short[g, 2:3, :] * ext[g, r + 6 : r + 6 + step, :]
            mixed.append(total)
        gate[r : r + step, :] = mixed[0]
        drive[r : r + step, :] = (mixed[1] * mixed[2]).astype(bf16)

    both_copy.wait()
    spec[...] = jnp.dot(both[...], drive[...], preferred_element_type=f32)

    for q in range(modes // 4):
        for lane in range(0, chans, 128):
            sums = [jnp.zeros((8, 128), f32) for _ in range(4)]
            for r in range(0, rows, 8):
                back_drive = spec[2 * rows + r : 2 * rows + r + 8, lane : lane + 128]
                for k in range(4):
                    sums[k] = sums[k] + powers[q * 4 + k, r : r + 8, lane : lane + 128] * back_drive
            for k in range(4):
                carry[q * 4 + k : q * 4 + k + 1, lane : lane + 128] = jnp.sum(sums[k], axis=0, keepdims=True)

    state_out[...] = carry[...].astype(bf16)
    states = []
    for rel in range(1, n_ctx):
        copy = remote(
            state_out,
            state_in.at[rel - 1],
            s_send.at[rel - 1],
            s_recv.at[rel - 1],
            {"ctx": lax.rem(ctx + rel, n_ctx)},
        )
        copy.start()
        states.append(copy)

    for r in range(0, rows, step):
        re, im = slice(r, r + step), slice(rows + r, rows + r + step)
        dr, di, kr, ki = spec[re, :], spec[im, :], spec_k[re, :], spec_k[im, :]
        spec[re, :] = dr * kr - di * ki
        spec[im, :] = dr * ki + di * kr
    back_copy.wait()
    conv[...] = jnp.dot(
        back[...], spec[0 : 2 * rows, :].astype(bf16), preferred_element_type=f32
    )

    block_decay = jnp.exp(-decay_all * rows)
    total = jnp.zeros((modes, chans), f32)
    for rel in range(n_ctx - 1, 0, -1):
        states[rel - 1].wait_recv()
        came = state_in[rel - 1].astype(f32)
        total = total * block_decay + came * jnp.where(ctx >= rel, 1.0, 0.0)
    carry[...] = total * amp[...] * jnp.exp(-decay_all)

    half = rows // 2
    shares = []
    for h in range(2):

        def tail(i, _, h=h):
            r = pl.multiple_of(h * half + i * 16, 16)
            here = pl.ds(r, 16)
            for lane in range(0, chans, 128):
                ln = slice(lane, lane + 128)
                total = conv[here, ln]
                for m in range(modes):
                    total = total + carry[m : m + 1, ln] * powers[m, here, ln]
                gated[here, ln] = (gate[here, ln] * total).astype(bf16)
            return 0

        lax.fori_loop(0, half // 16, tail, 0)
        share = remote(
            gated.at[h * half : (h + 1) * half],
            gated_in.at[h * half : (h + 1) * half],
            r_send.at[h],
            r_recv.at[h],
            {"chan": sib},
        )
        share.start()
        shares.append(share)

    for copy in ow_copies:
        copy.wait()
    for copy in ow_out:
        copy.wait_recv()
    wide = width // 2
    results = []
    for h in range(2):
        shares[h].wait_recv()
        hr = slice(h * half, (h + 1) * half)
        for j in range(2):
            jc = slice(j * wide, (j + 1) * wide)
            k = h * 2 + j
            part = jnp.dot(gated[hr, :], ow[0, 1, :, jc], preferred_element_type=f32)
            part = part + jnp.dot(gated_in[hr, :], ow[1, 1, :, jc], preferred_element_type=f32)
            sent[hr, jc] = part.astype(bf16)
            copy = remote(
                sent.at[hr, jc], landed.at[hr, jc], r_send.at[2 + k], r_recv.at[2 + k], {"chan": acr}
            )
            copy.start()
            results.append(copy)
    for j in range(2):
        jc = slice(j * wide, (j + 1) * wide)
        kept = jnp.dot(gated[...], ow[0, 0, :, jc], preferred_element_type=f32)
        kept = kept + jnp.dot(gated_in[...], ow[1, 0, :, jc], preferred_element_type=f32)
        acc[j, 0:rows, :] = kept
    for h in range(2):
        hr = slice(h * half, (h + 1) * half)
        for j in range(2):
            jc = slice(j * wide, (j + 1) * wide)
            results[h * 2 + j].wait_recv()
            out[hr, jc] = (acc[j, hr, :] + landed[hr, jc].astype(f32)).astype(bf16)

    for copy in across + onward + states + shares + results + ow_out:
        copy.wait_send()
    for copy in (beside, rim_on, rim_across, rim_beside, rim_onward):
        copy.wait_send()


def shards(n_ctx, tokens, gain, in_weight, short_weight, residues, rates, out_weight):
    rows, width = tokens.shape
    chans = in_weight.shape[2]
    modes = rates.shape[0]
    forward, both, backward = tables(rows)
    tall = rows + RIM
    vmem = pl.BlockSpec(memory_space=pltpu.VMEM)
    hbm = pl.BlockSpec(memory_space=pl.ANY)
    dma = pltpu.SemaphoreType.DMA
    return pl.pallas_call(
        functools.partial(layer, n_ctx),
        out_shape=jax.ShapeDtypeStruct((rows, width), bf16),
        in_specs=[hbm, vmem, hbm, vmem, vmem, vmem, hbm, hbm, hbm, hbm],
        out_specs=vmem,
        scratch_shapes=[
            pltpu.VMEM((4, tall, width), bf16),
            pltpu.VMEM((3, 4 * width, chans), bf16),
            pltpu.VMEM((2, 2, chans, width), bf16),
            pltpu.VMEM((2 * rows, rows), f32),
            pltpu.VMEM((3 * rows, rows), bf16),
            pltpu.VMEM((rows, 2 * rows), bf16),
            pltpu.VMEM((3, tall, chans), f32),
            pltpu.VMEM((tall, 128), f32),
            pltpu.VMEM((3, rows + 8, chans), f32),
            pltpu.VMEM((rows, chans), f32),
            pltpu.VMEM((modes, rows, chans), f32),
            pltpu.VMEM((2 * rows, chans), f32),
            pltpu.VMEM((3 * rows, chans), f32),
            pltpu.VMEM((rows, chans), bf16),
            pltpu.VMEM((rows, chans), f32),
            pltpu.VMEM((modes, chans), f32),
            pltpu.VMEM((modes, chans), bf16),
            pltpu.VMEM((n_ctx - 1, modes, chans), bf16),
            pltpu.VMEM((modes, chans), f32),
            pltpu.VMEM((rows, chans), bf16),
            pltpu.VMEM((rows, chans), bf16),
            pltpu.VMEM((rows, width), bf16),
            pltpu.VMEM((rows, width), bf16),
            dma((10,)),
            dma((9,)),
            dma((9,)),
            dma((4,)),
            dma((4,)),
            dma((2,)),
            dma((2,)),
            dma((n_ctx - 1,)),
            dma((n_ctx - 1,)),
            dma((6,)),
            dma((6,)),
        ],
        compiler_params=pltpu.CompilerParams(
            collective_id=0, has_side_effects=True, vmem_limit_bytes=60 * 1024 * 1024
        ),
        name="hyena_layer",
    )(
        tokens,
        gain.reshape(4, width),
        in_weight,
        short_weight,
        residues,
        rates,
        out_weight,
        jnp.asarray(forward),
        jnp.asarray(both, dtype=bf16),
        jnp.asarray(backward, dtype=bf16),
    )


def solution(mesh):
    return jax.shard_map(
        functools.partial(shards, mesh.shape["ctx"]),
        mesh=mesh,
        in_specs=(
            P("ctx", "chan"),
            P(),
            P(None, None, "chan"),
            P(None, None, "chan"),
            P(None, "chan"),
            P(None, "chan"),
            P("chan", None),
        ),
        out_specs=P("ctx", "chan"),
        check_vma=False,
    )
```

```python
import functools
import math

import jax
import jax.numpy as jnp
import numpy as np
from jax import lax
from jax.experimental import pallas as pl
from jax.experimental.pallas import tpu as pltpu
from jax.sharding import PartitionSpec as P

RIM = 16
MESH = pl.DeviceIdType.MESH
f32 = jnp.float32
bf16 = jnp.bfloat16


def tables(rows):
    steps = np.arange(rows)
    turns = ((2 * steps[:, None] + 1) * steps[None, :]) % (4 * rows)
    angle = turns * (math.pi / (2 * rows))
    cos, sin = np.cos(angle), np.sin(angle)
    forward = np.concatenate([cos, -sin], axis=0)
    flipped = np.eye(rows)[::-1]
    both = np.concatenate([forward, flipped], axis=0)
    backward = np.concatenate([cos.T, -sin.T], axis=1) / rows
    return forward.astype(np.float32), both.astype(np.float32), backward.astype(np.float32)


def one_less_exp(x):
    series = jnp.full_like(x, 1.0 / 5040.0)
    for term in (720.0, 120.0, 24.0, 6.0, 2.0, 1.0):
        series = 1.0 / term - x * series
    return jnp.where(x < 0.25, x * series, 1.0 - jnp.exp(-x))


def layer(
    n_ctx,
    tok,
    gain,
    w_hbm,
    short,
    residues,
    rates,
    ow_hbm,
    fwd_hbm,
    both_hbm,
    back_hbm,
    out,
    buf,
    w,
    ow,
    fwd,
    both,
    back,
    acc,
    squares,
    ext,
    gate,
    powers,
    spec_k,
    spec,
    drive,
    conv,
    amp,
    state_out,
    state_in,
    carry,
    gated,
    gated_in,
    sent,
    landed,
    local_sem,
    g_send,
    g_recv,
    h_send,
    h_recv,
    o_send,
    o_recv,
    s_send,
    s_recv,
    r_send,
    r_recv,
    near_sem,
):
    rows, width = tok.shape
    chans = w_hbm.shape[2]
    modes = rates.shape[0]
    cut = width // 4
    length = rows * n_ctx
    me = lax.axis_index("chan")
    ctx = lax.axis_index("ctx")
    sib = me + 1 - 2 * lax.rem(me, 2)
    acr = lax.rem(me + 2, 4)
    dia = lax.rem(sib + 2, 4)
    owners = (me, sib, acr, dia)

    def local(src, dst, k):
        copy = pltpu.make_async_copy(src, dst, local_sem.at[k])
        copy.start()
        return copy

    def remote(src, dst, send, recv, peer):
        return pltpu.make_async_remote_copy(
            src_ref=src, dst_ref=dst, send_sem=send, recv_sem=recv, device_id=peer, device_id_type=MESH
        )

    def cols(block, size):
        return pl.ds(pl.multiple_of(block * size, size), size)

    def greet(sem, far):
        @pl.when(ctx + far < n_ctx)
        def _():
            pl.semaphore_signal(sem, inc=1, device_id={"ctx": ctx + far}, device_id_type=MESH)

        @pl.when(ctx >= far)
        def _():
            pl.semaphore_signal(sem, inc=1, device_id={"ctx": ctx - far}, device_id_type=MESH)

    def meet(sem, far, others=0):
        ahead = 1 - lax.div(ctx + far, n_ctx)
        behind = lax.div(ctx + n_ctx - far, n_ctx)
        pl.semaphore_wait(sem, others + ahead + behind)

    own_tokens = local(tok, buf.at[0, 0:rows], 0)
    fwd_copy = local(fwd_hbm, fwd, 1)
    w_copies = [
        local(w_hbm.at[:, cols(owners[s], width), :], w.at[:, s * width : (s + 1) * width, :], 2 + s)
        for s in range(4)
    ]
    both_copy = local(both_hbm, both, 6)
    back_copy = local(back_hbm, back, 7)
    ow_copies = [local(ow_hbm.at[:, cols(b, width)], ow.at[0, i], 8 + i) for i, b in enumerate((me, acr))]

    barrier = pltpu.get_barrier_semaphore()
    pl.semaphore_signal(barrier, inc=1, device_id={"chan": sib}, device_id_type=MESH)
    pl.semaphore_signal(barrier, inc=1, device_id={"chan": acr}, device_id_type=MESH)
    greet(barrier, 1)
    meet(barrier, 1, 2)

    reach = []
    while sum(reach) + 1 < n_ctx - 1:
        reach.append(2 ** len(reach))

    def widen(k):
        if 0 <= k - 1 < len(reach):
            meet(near_sem.at[k - 1], reach[k - 1])
        if k < len(reach):
            greet(near_sem.at[k], reach[k])

    widen(0)

    across = []
    for c in range(4):
        here = slice(c * cut, (c + 1) * cut)
        across.append(
            remote(tok.at[:, here], buf.at[2, 0:rows, here], g_send.at[c], g_recv.at[c], {"chan": acr})
        )
    beside = remote(tok, buf.at[1, 0:rows], g_send.at[4], g_recv.at[4], {"chan": sib})
    rim_on = remote(
        tok.at[rows - RIM : rows, :],
        buf.at[0, rows : rows + RIM],
        h_send.at[0],
        h_recv.at[0],
        {"ctx": lax.rem(ctx + 1, n_ctx)},
    )

    @pl.when(ctx + 1 < n_ctx)
    def _():
        rim_on.start()

    across[0].start()
    beside.start()
    rim_here = buf.at[0, rows : rows + RIM]

    @pl.when(ctx > 0)
    def _():
        rim_on.wait_recv()

    @pl.when(ctx == 0)
    def _():
        buf[0, rows : rows + RIM] = jnp.zeros((RIM, width), bf16)

    rim_across = remote(rim_here, buf.at[2, rows : rows + RIM], h_send.at[1], h_recv.at[1], {"chan": acr})
    rim_beside = remote(rim_here, buf.at[1, rows : rows + RIM], h_send.at[2], h_recv.at[2], {"chan": sib})
    rim_across.start()
    rim_beside.start()
    for c in range(1, 4):
        across[c].start()
    ow_out = []
    for i, b in enumerate((sib, dia)):
        copy = remote(ow_hbm.at[:, cols(b, width)], ow.at[1, i], o_send.at[i], o_recv.at[i], {"chan": sib})
        copy.start()
        ow_out.append(copy)

    decay_all = rates[...] * (1.0 / length)
    amp[...] = residues[...] * jnp.sqrt(one_less_exp(2.0 * decay_all))
    conv[...] = jnp.zeros_like(conv)
    eighth = lax.broadcasted_iota(jnp.int32, (8, chans), 0).astype(f32)
    groups = lax.broadcasted_iota(jnp.int32, (rows // 8, chans), 0).astype(f32) * 8.0

    def build(m, _):
        decay = rates[pl.ds(m, 1), :] * (1.0 / length)
        fine = jnp.exp(-decay * eighth)
        coarse = jnp.exp(-decay * groups)
        strength = amp[pl.ds(m, 1), :]
        for a in range(rows // 8):
            here = slice(a * 8, a * 8 + 8)
            value = fine * coarse[a : a + 1, :]
            powers[m, here, :] = value
            conv[here, :] += strength * value
        return 0

    lax.fori_loop(0, modes, build, 0)
    widen(1)

    squares[...] = jnp.zeros_like(squares)

    def accumulate(slot, start, size, first):
        x = buf[slot, :, start : start + size].astype(f32)
        part = squares[...]
        for k in range(0, size, 128):
            piece = x[:, k : k + 128]
            part = part + piece * piece
        squares[...] = part
        scaled = (x * gain[cols(owners[slot] * (width // size) + start // size, size)][None, :]).astype(bf16)
        for g in range(3):
            base = slot * width + start
            term = jnp.dot(scaled, w[g, base : base + size, :], preferred_element_type=f32)
            if first:
                acc[g] = term
            else:
                acc[g] += term

    own_tokens.wait()
    w_copies[0].wait()
    accumulate(0, 0, width, True)
    widen(2)
    across[0].wait_recv()
    onward = [
        remote(
            buf.at[2, 0:rows, c * cut : (c + 1) * cut],
            buf.at[3, 0:rows, c * cut : (c + 1) * cut],
            g_send.at[5 + c],
            g_recv.at[5 + c],
            {"chan": sib},
        )
        for c in range(4)
    ]
    onward[0].start()
    rim_across.wait_recv()
    rim_onward = remote(
        buf.at[2, rows : rows + RIM], buf.at[3, rows : rows + RIM], h_send.at[3], h_recv.at[3], {"chan": sib}
    )
    rim_onward.start()
    rim_beside.wait_recv()
    beside.wait_recv()
    w_copies[1].wait()
    accumulate(1, 0, width, False)
    widen(3)

    fwd_copy.wait()
    spec_k[...] = jnp.dot(
        fwd[...], conv[...], preferred_element_type=f32, precision=lax.Precision.HIGHEST
    )

    w_copies[2].wait()
    w_copies[3].wait()
    for c in range(4):
        if c:
            across[c].wait_recv()
            onward[c].start()
        accumulate(2, c * cut, cut, False)
        if c == 0:
            rim_onward.wait_recv()
        onward[c].wait_recv()
        accumulate(3, c * cut, cut, False)
        widen(4 + c)

    mean = jnp.sum(squares[...], axis=1, keepdims=True) * (1.0 / (4 * width))
    scale = lax.rsqrt(mean + 1e-06)
    keep = jnp.where(ctx > 0, 1.0, 0.0)
    for g in range(3):
        ext[g, 0:8, :] = (acc[g, rows + 8 : rows + 16, :] * scale[rows + 8 : rows + 16]).astype(bf16).astype(
            f32
        ) * keep
        ext[g, 8 : rows + 8, :] = (acc[g, 0:rows, :] * scale[0:rows]).astype(bf16).astype(f32)
    step = 64
    for r in range(0, rows, step):
        mixed = []
        for g in range(3):
            total = short[g, 0:1, :] * ext[g, r + 8 : r + 8 + step, :]
            total = total + short[g, 1:2, :] * ext[g, r + 7 : r + 7 + step, :]
            total = total + short[g, 2:3, :] * ext[g, r + 6 : r + 6 + step, :]
            mixed.append(total)
        gate[r : r + step, :] = mixed[0]
        drive[r : r + step, :] = (mixed[1] * mixed[2]).astype(bf16)

    both_copy.wait()
    spec[...] = jnp.dot(both[...], drive[...], preferred_element_type=f32)

    for q in range(modes // 4):
        for lane in range(0, chans, 128):
            sums = [jnp.zeros((8, 128), f32) for _ in range(4)]
            for r in range(0, rows, 8):
                back_drive = spec[2 * rows + r : 2 * rows + r + 8, lane : lane + 128]
                for k in range(4):
                    sums[k] = sums[k] + powers[q * 4 + k, r : r + 8, lane : lane + 128] * back_drive
            for k in range(4):
                carry[q * 4 + k : q * 4 + k + 1, lane : lane + 128] = jnp.sum(sums[k], axis=0, keepdims=True)

    state_out[...] = carry[...].astype(bf16)
    states = []
    for rel in range(1, n_ctx):
        copy = remote(
            state_out,
            state_in.at[rel - 1],
            s_send.at[rel - 1],
            s_recv.at[rel - 1],
            {"ctx": lax.rem(ctx + rel, n_ctx)},
        )
        states.append(copy)

        @pl.when(ctx + rel < n_ctx)
        def _(copy=copy):
            copy.start()


    for r in range(0, rows, step):
        re, im = slice(r, r + step), slice(rows + r, rows + r + step)
        dr, di, kr, ki = spec[re, :], spec[im, :], spec_k[re, :], spec_k[im, :]
        spec[re, :] = dr * kr - di * ki
        spec[im, :] = dr * ki + di * kr
    back_copy.wait()
    conv[...] = jnp.dot(
        back[...], spec[0 : 2 * rows, :].astype(bf16), preferred_element_type=f32
    )

    block_decay = jnp.exp(-decay_all * rows)
    carry[...] = jnp.zeros_like(carry)
    for rel in range(n_ctx - 1, 0, -1):
        @pl.when(ctx >= rel)
        def _(rel=rel):
            states[rel - 1].wait_recv()
            came = state_in[rel - 1].astype(f32)
            carry[...] = carry[...] * block_decay + came

    carry[...] = carry[...] * amp[...] * jnp.exp(-decay_all)

    half = rows // 2
    shares = []
    for h in range(2):

        def tail(i, _, h=h):
            r = pl.multiple_of(h * half + i * 16, 16)
            here = pl.ds(r, 16)
            for lane in range(0, chans, 128):
                ln = slice(lane, lane + 128)
                total = conv[here, ln]
                for m in range(modes):
                    total = total + carry[m : m + 1, ln] * powers[m, here, ln]
                gated[here, ln] = (gate[here, ln] * total).astype(bf16)
            return 0

        lax.fori_loop(0, half // 16, tail, 0)
        share = remote(
            gated.at[h * half : (h + 1) * half],
            gated_in.at[h * half : (h + 1) * half],
            r_send.at[h],
            r_recv.at[h],
            {"chan": sib},
        )
        share.start()
        shares.append(share)

    for copy in ow_copies:
        copy.wait()
    for copy in ow_out:
        copy.wait_recv()
    wide = width // 2
    results = []
    for h in range(2):
        shares[h].wait_recv()
        hr = slice(h * half, (h + 1) * half)
        for j in range(2):
            jc = slice(j * wide, (j + 1) * wide)
            k = h * 2 + j
            part = jnp.dot(gated[hr, :], ow[0, 1, :, jc], preferred_element_type=f32)
            part = part + jnp.dot(gated_in[hr, :], ow[1, 1, :, jc], preferred_element_type=f32)
            sent[hr, jc] = part.astype(bf16)
            copy = remote(
                sent.at[hr, jc], landed.at[hr, jc], r_send.at[2 + k], r_recv.at[2 + k], {"chan": acr}
            )
            copy.start()
            results.append(copy)
    for j in range(2):
        jc = slice(j * wide, (j + 1) * wide)
        kept = jnp.dot(gated[...], ow[0, 0, :, jc], preferred_element_type=f32)
        kept = kept + jnp.dot(gated_in[...], ow[1, 0, :, jc], preferred_element_type=f32)
        acc[j, 0:rows, :] = kept
    for h in range(2):
        hr = slice(h * half, (h + 1) * half)
        for j in range(2):
            jc = slice(j * wide, (j + 1) * wide)
            results[h * 2 + j].wait_recv()
            out[hr, jc] = (acc[j, hr, :] + landed[hr, jc].astype(f32)).astype(bf16)

    for copy in across + onward + shares + results + ow_out:
        copy.wait_send()
    for copy in (beside, rim_across, rim_beside, rim_onward):
        copy.wait_send()
    for rel in range(1, n_ctx):

        @pl.when(ctx + rel < n_ctx)
        def _(rel=rel):
            states[rel - 1].wait_send()
            if rel == 1:
                rim_on.wait_send()


def shards(n_ctx, tokens, gain, in_weight, short_weight, residues, rates, out_weight):
    rows, width = tokens.shape
    chans = in_weight.shape[2]
    modes = rates.shape[0]
    forward, both, backward = tables(rows)
    tall = rows + RIM
    vmem = pl.BlockSpec(memory_space=pltpu.VMEM)
    hbm = pl.BlockSpec(memory_space=pl.ANY)
    dma = pltpu.SemaphoreType.DMA
    return pl.pallas_call(
        functools.partial(layer, n_ctx),
        out_shape=jax.ShapeDtypeStruct((rows, width), bf16),
        in_specs=[hbm, vmem, hbm, vmem, vmem, vmem, hbm, hbm, hbm, hbm],
        out_specs=vmem,
        scratch_shapes=[
            pltpu.VMEM((4, tall, width), bf16),
            pltpu.VMEM((3, 4 * width, chans), bf16),
            pltpu.VMEM((2, 2, chans, width), bf16),
            pltpu.VMEM((2 * rows, rows), f32),
            pltpu.VMEM((3 * rows, rows), bf16),
            pltpu.VMEM((rows, 2 * rows), bf16),
            pltpu.VMEM((3, tall, chans), f32),
            pltpu.VMEM((tall, 128), f32),
            pltpu.VMEM((3, rows + 8, chans), f32),
            pltpu.VMEM((rows, chans), f32),
            pltpu.VMEM((modes, rows, chans), f32),
            pltpu.VMEM((2 * rows, chans), f32),
            pltpu.VMEM((3 * rows, chans), f32),
            pltpu.VMEM((rows, chans), bf16),
            pltpu.VMEM((rows, chans), f32),
            pltpu.VMEM((modes, chans), f32),
            pltpu.VMEM((modes, chans), bf16),
            pltpu.VMEM((n_ctx - 1, modes, chans), bf16),
            pltpu.VMEM((modes, chans), f32),
            pltpu.VMEM((rows, chans), bf16),
            pltpu.VMEM((rows, chans), bf16),
            pltpu.VMEM((rows, width), bf16),
            pltpu.VMEM((rows, width), bf16),
            dma((10,)),
            dma((9,)),
            dma((9,)),
            dma((4,)),
            dma((4,)),
            dma((2,)),
            dma((2,)),
            dma((n_ctx - 1,)),
            dma((n_ctx - 1,)),
            dma((6,)),
            dma((6,)),
            pltpu.SemaphoreType.REGULAR((8,)),
        ],
        compiler_params=pltpu.CompilerParams(
            collective_id=0, has_side_effects=True, vmem_limit_bytes=60 * 1024 * 1024
        ),
        name="hyena_layer",
    )(
        tokens,
        gain,
        in_weight,
        short_weight,
        residues,
        rates,
        out_weight,
        jnp.asarray(forward),
        jnp.asarray(both, dtype=bf16),
        jnp.asarray(backward, dtype=bf16),
    )


def solution(mesh):
    return jax.shard_map(
        functools.partial(shards, mesh.shape["ctx"]),
        mesh=mesh,
        in_specs=(
            P("ctx", "chan"),
            P(),
            P(None, None, "chan"),
            P(None, None, "chan"),
            P(None, "chan"),
            P(None, "chan"),
            P("chan", None),
        ),
        out_specs=P("ctx", "chan"),
        check_vma=False,
    )
```
